128 devices in a mesh: gx: 8 (over x_hi, z), gy: 16 (over y, x_lo, core).
Axes of the slice: x: 4 (x_hi: 2, x_lo: 2; x = x_hi * 2 + x_lo), y: 4, z: 4, core: 2. Of those that a mesh axis runs over, the one named last changes fastest.
Arguments:
- state: float32 [10, 32, 131072], P(None, None, ('gx', 'gy'))
- kdist: bfloat16 [224, 32], replicated, may hold values from 9.9658966e-05 to 0.049804688
- rayleigh: float32 [224], replicated, may hold values from 0.002 to 0.05
- solar: float32 [224], replicated, may hold values from 0.002 to 0.01
- span_map: int32 [131072], P(('gx', 'gy')), may hold values from 0 to 131071, as said below
- cos_zenith: float32 [131072], P(('gx', 'gy')), may hold values from -1 to 1, as said below
- day_flag: int32 [131072], P(('gx', 'gy')), may hold values from 0 to 1, as said below
- albedo: float32 [131072], P(('gx', 'gy')), may hold values from 0.05 to 0.8
Outputs:
- heating: float32 [32, 131072], P(None, ('gx', 'gy'))
- surface: float32 [3, 131072], P(None, ('gx', 'gy'))
The draws below stay inside these ranges and needn't reach their ends.
Inputs may be any that keep to these rules, and one draw needn't show every extreme that they name: span_map is a permutation of the 131072 columns; a column held by device s (index in gx+gy order) goes to a column p with (p % 1024) // 8 == s, and each device's columns reach every device equally often. `cos_zenith`: column j of device d (index in gx+gy order) and column 1023 - j of the device whose index differs from d by 64 are antipodes: their values are opposite, of magnitude 0.05 or more. `day_flag`: 1 exactly where cos_zenith > 0.
All inputs are finite; a program needn't handle non-finite values.
Results may differ from the reference program's by a relative error of at most 0.00069.
Values sent between devices are 32-bit elements; how exact they have to be, the bound alone decides.
No kernel may reach another device: no remote copies, remote signals or barrier semaphores. Data moves between devices by JAX's collectives and lax.ppermute only.
A program may use at most 64 MiB of HBM per device.

```python
import math
import jax
import jax.numpy as jnp
from jax import lax

G = 224
NGAS = 8
NLEV = 32
COLS_DEV = 1024
NPRED = 32
NCOL = 131072
N_GX = 8
N_GY = 16


def antipode_signs(key):
    devices = N_GX * N_GY
    lower_count = devices // 2
    initial_height_index, second = jax.random.split(jax.random.fold_in(key, 7))
    levels = jax.random.randint(initial_height_index, (lower_count, 1), 1, 8)
    draws = jax.random.randint(second, (lower_count, COLS_DEV), 0, 8)
    lower_half = jnp.where(draws < levels, 1, -1).astype(jnp.int32)
    upper_half = -lower_half[:, ::-1]
    return jnp.concatenate([lower_half, upper_half], 0).reshape(-1)


def draw_day_flag(key, part):
    signs = antipode_signs(key)
    return jnp.where(signs > 0, 1, 0).astype(jnp.int32)


def draw_cos_zenith(key, part):
    signs = antipode_signs(key).astype(jnp.float32)
    devices = N_GX * N_GY
    uniform_part = jax.random.uniform(jax.random.fold_in(key, 9), (devices // 2, COLS_DEV), jnp.float32)
    magnitude = 0.05 + 0.95 * uniform_part
    full = jnp.concatenate([magnitude, magnitude[:, ::-1]], 0).reshape(-1)
    return (signs * full).astype(jnp.float32)


def draw_span_map(key, part):
    devices = N_GX * N_GY
    per_peer = COLS_DEV // devices
    keys = jax.random.split(jax.random.fold_in(key, 5), devices)
    orders = jax.vmap(lambda single: jax.random.permutation(single, COLS_DEV))(keys).astype(jnp.int32)
    source = jnp.arange(devices, dtype=jnp.int32)[:, None]
    target = orders // per_peer * COLS_DEV + source * per_peer + orders % per_peer
    return target.reshape(-1).astype(jnp.int32)


def draw_state(key, part):
    initial_height_index, second, third = jax.random.split(jax.random.fold_in(key, 11), 3)
    dimension_tuple = (NLEV, NCOL)
    kelvin_profile = jax.random.uniform(initial_height_index, dimension_tuple, jnp.float32, 190.0, 310.0)
    slab_weight_per_area = jnp.exp(jax.random.uniform(second, dimension_tuple, jnp.float32, -1.2, 1.1))
    absorber_columns = jnp.exp(jax.random.uniform(third, (NGAS, NLEV, NCOL), jnp.float32, -4.6, 0.0))
    return jnp.concatenate([kelvin_profile[None], slab_weight_per_area[None], absorber_columns], 0).astype(jnp.float32)


def block_scale(key, extent, cuts, least, high):
    factor_of, own = 1.0, jax.random.fold_in(key, 6)
    for dim, shards_of in cuts:
        steps = jnp.exp(jax.random.uniform(jax.random.fold_in(own, dim), (shards_of,), jnp.float32, least / len(cuts), high / len(cuts)))
        factor_of = factor_of * jnp.repeat(steps, extent[dim] // shards_of).reshape([-1 if axis == dim else 1 for axis in range(len(extent))])
    return factor_of


def setup_inputs(seed: int = 0) -> dict:
    key_of = jax.random.split(jax.random.key(seed), 9)
    return {
        "state": draw_state(jax.random.fold_in(key_of[8], 71), 0),
        "kdist": jnp.clip(jnp.exp(jax.random.uniform(key_of[1], (G, NPRED), jnp.float32, math.log(9.965896606445312e-05), math.log(0.049804688))), 9.965896606445312e-05, 0.049804688).astype(jnp.bfloat16),
        "rayleigh": jnp.clip(jnp.exp(jax.random.uniform(key_of[2], (G,), jnp.float32, math.log(0.002), math.log(0.05))), 0.002, 0.05),
        "solar": jnp.clip(jnp.exp(jax.random.uniform(key_of[3], (G,), jnp.float32, math.log(0.002), math.log(0.01))), 0.002, 0.01),
        "span_map": draw_span_map(jax.random.fold_in(key_of[8], 71), 0),
        "cos_zenith": draw_cos_zenith(jax.random.fold_in(key_of[8], 71), 0),
        "day_flag": draw_day_flag(jax.random.fold_in(key_of[8], 71), 0),
        "albedo": jnp.clip(0.05 + 0.75 * jax.random.uniform(key_of[7], (NCOL,), jnp.float32) ** block_scale(key_of[7], (NCOL,), ((0, 128),), -0.2, 0.2), 0.05, 0.8),
    }


diffusivity = 1.66
heat_factor = 8.0


def upward(carried, layer):
    albedo_below, source_below = carried
    reflect, transmit, direct_src = layer
    divisor = 1.0 - reflect * albedo_below
    albedo_top = reflect + transmit * transmit * albedo_below / divisor
    source_top = direct_src + transmit * (source_below + albedo_below * direct_src) / divisor
    return (albedo_top, source_top), (albedo_below, source_below)


def downward(diffuse, layer):
    reflect, transmit, direct_src, albedo_below, source_below = layer
    lower_down = (transmit * diffuse + direct_src + reflect * source_below) / (1.0 - reflect * albedo_below)
    lower_up = albedo_below * lower_down + source_below
    return lower_down, (lower_down, lower_up)


def column_physics(quantity_bundle, cosine, albedo, kdist, rayleigh, solar):
    levels = quantity_bundle.shape[1]
    columns = quantity_bundle.shape[2]
    kelvin_profile = quantity_bundle[0] / 250.0
    slab_weight_per_area = quantity_bundle[1]
    expansion_modes = jnp.stack([jnp.ones_like(kelvin_profile), kelvin_profile, kelvin_profile * kelvin_profile, 1.0 / kelvin_profile])
    predictors = (quantity_bundle[2:, None] * expansion_modes[None] * slab_weight_per_area).astype(jnp.bfloat16)
    predictors = predictors.reshape(-1, levels, columns)
    block_width = math.gcd(kdist.shape[0], 32)
    blocks = kdist.shape[0] // block_width

    def one_block(block_index):
        start = block_index * block_width
        k_rows = lax.dynamic_slice_in_dim(kdist, start, block_width, 0)
        ray_rows = lax.dynamic_slice_in_dim(rayleigh, start, block_width, 0)
        sun_rows = lax.dynamic_slice_in_dim(solar, start, block_width, 0)
        tau_gas = jnp.einsum("gp,plc->lgc", k_rows.astype(jnp.float32), predictors.astype(jnp.float32), precision=lax.Precision.HIGHEST)
        tau_ray = ray_rows[None, :, None] * slab_weight_per_area[:, None, :]
        optical = tau_gas + tau_ray
        albedo_single = tau_ray / optical
        extinct = jnp.exp(-diffusivity * optical)
        reflect = 0.5 * albedo_single * (1.0 - extinct)
        transmit = extinct + reflect
        cumulative = jnp.cumsum(optical, axis=0)
        above = cumulative - optical
        direct_top = sun_rows[None, :, None] * cosine * jnp.exp(-above / cosine)
        direct_bottom = sun_rows[:, None] * cosine * jnp.exp(-cumulative[-1] / cosine)
        direct_src = 0.5 * albedo_single * (1.0 - jnp.exp(-optical / cosine)) * direct_top
        start_albedo = jnp.broadcast_to(albedo, direct_bottom.shape)
        (albedo_end, source_top), (albedo_below, source_below) = lax.scan(upward, (start_albedo, albedo * direct_bottom), (reflect, transmit, direct_src), reverse=True)
        zeros = jnp.zeros_like(direct_bottom)
        final_down, (lower_down, lower_up) = lax.scan(downward, zeros, (reflect, transmit, direct_src, albedo_below, source_below))
        direct_all = jnp.concatenate([direct_top, direct_bottom[None]], 0)
        down_all = jnp.concatenate([zeros[None], lower_down], 0)
        up_all = jnp.concatenate([source_top[None], lower_up], 0)
        net = jnp.sum(direct_all + down_all - up_all, axis=1)
        surface = jnp.stack([jnp.sum(direct_bottom, 0), jnp.sum(final_down, 0), jnp.sum(source_top, 0)])
        return net, surface

    nets, surfaces = lax.map(one_block, jnp.arange(blocks, dtype=jnp.int32))
    net = jnp.sum(nets, 0)
    heat_rate = heat_factor * (net[:-1] - net[1:]) / slab_weight_per_area
    return heat_rate, jnp.sum(surfaces, 0)


def reference(state, kdist, rayleigh, solar, span_map, cos_zenith, day_flag, albedo):
    spanned = jnp.zeros_like(state).at[:, :, span_map].set(state)
    groups = spanned.shape[-1] // COLS_DEV
    daylit = day_flag.astype(jnp.float32)
    cosine_all = jnp.where(day_flag == 1, cos_zenith, jnp.float32(1.0))

    def one_group(group_index):
        start = group_index * COLS_DEV
        quantity_bundle = lax.dynamic_slice_in_dim(spanned, start, COLS_DEV, 2)
        cosine = lax.dynamic_slice_in_dim(cosine_all, start, COLS_DEV, 0)
        ground = lax.dynamic_slice_in_dim(albedo, start, COLS_DEV, 0)
        mask = lax.dynamic_slice_in_dim(daylit, start, COLS_DEV, 0)
        heat_rate, surface = column_physics(quantity_bundle, cosine, ground, kdist, rayleigh, solar)
        return heat_rate * mask, surface * mask

    heat_rate, surface = lax.map(one_group, jnp.arange(groups, dtype=jnp.int32))
    heat_span = jnp.moveaxis(heat_rate, 0, 1).reshape(NLEV, -1)
    surface = jnp.moveaxis(surface, 0, 1).reshape(3, -1)
    heating = jnp.take(heat_span, span_map, axis=1)
    return heating, surface
```

```python
import jax
import jax.numpy as jnp
from jax import lax
from jax.experimental import pallas as pl
from jax.experimental.pallas import tpu as pltpu
from jax.sharding import PartitionSpec as P

AXES = ("gx", "gy")
F32 = jnp.float32
BF16 = jnp.bfloat16
LOG2E = 1.4426950408889634
DIFFUSIVITY = 1.66
HEAT_FACTOR = 8.0
LANES = 128
HALF = 64
CHUNK = 256


def split3(x):
    hi = x.astype(BF16)
    rest = x - hi.astype(F32)
    mid = rest.astype(BF16)
    low = (rest - mid.astype(F32)).astype(BF16)
    return hi, mid, low


def dot(a, b, dims=((1,), (0,))):
    return lax.dot_general(a, b, (dims, ((), ())), preferred_element_type=F32)


def iota(shape, dim):
    return lax.broadcasted_iota(jnp.int32, shape, dim)


def send_kernel(cos_ref, day_ref, alb_ref, out_ref):
    rows = cos_ref.shape[0]
    devices = out_ref.shape[0]
    group = devices // rows
    per = LANES // group
    keep = iota((devices, LANES), 1) // per == iota((devices, LANES), 0) % group
    cosine = jnp.where(day_ref[...] == 1, cos_ref[...], 0.0)

    def spread(x):
        x = jnp.broadcast_to(x[:, None, :], (rows, group, LANES)).reshape(devices, LANES)
        return jnp.where(keep, x, 0.0)

    out_ref[...] = spread(cosine) + pltpu.roll(spread(alb_ref[...]), per, 1)


def main_kernel(
    shift_ref,
    state_ref,
    recv_ref,
    span_ref,
    lhs_ref,
    rayh_ref,
    sun_ref,
    heat_ref,
    send_ref,
    pred_s,
    gather_s,
    pick_s,
    tau_s,
    trans_s,
    emit_s,
    back_s,
    net_s,
    sfc_s,
    mass_s,
    out_s,
    fin_s,
):
    levels, columns = state_ref.shape[1:]
    gases = state_ref.shape[0] - 2
    npred = 4 * gases
    devices = recv_ref.shape[0]
    per = columns // devices
    grows = rayh_ref.shape[0]
    base = npred * levels
    tail = base + 3 * levels
    gtail = base + 8 * levels

    t = state_ref[0] / 250.0
    m = state_ref[1]
    modes = (None, t, t * t, 1.0 / t)
    for i in range(gases):
        q = state_ref[2 + i]
        for b in range(4):
            v = (q if b == 0 else q * modes[b]) * m
            pred_s[pl.ds((4 * i + b) * levels, levels), :] = v.astype(BF16)
    for j, term in enumerate(split3(m)):
        pred_s[pl.ds(base + j * levels, levels), :] = term

    span = span_ref[...]

    def owner_hot():
        return jnp.where(iota((devices, columns), 0) == span // columns, 1.0, 0.0).astype(BF16)

    slot_hot = iota((per, columns), 0) == span % per
    recv = pltpu.roll(recv_ref[...], shift_ref[0], 1).T[: 2 * per]
    sel = dot(jnp.concatenate(split3(recv), 0), owner_hot())
    sel = sel[: 2 * per] + sel[2 * per : 4 * per] + sel[4 * per :]
    cos_e = jnp.sum(jnp.where(slot_hot, sel[:per], 0.0), 0, keepdims=True)
    alb_e = jnp.sum(jnp.where(slot_hot, sel[per:], 0.0), 0, keepdims=True)
    extra = [x.astype(F32) for x in (*split3(cos_e), *split3(alb_e))]
    extra = jnp.concatenate(extra + [jnp.zeros((10, columns), F32)], 0)
    pred_s[pl.ds(tail, 16), :] = extra.astype(BF16)

    day = jnp.where(cos_e > 0.0, 1.0, 0.0)
    rows = columns // LANES
    day2 = jnp.concatenate([day[:, r * LANES : (r + 1) * LANES] for r in range(rows)], 0)
    upper = jnp.where(iota((LANES, LANES), 0) <= iota((LANES, LANES), 1), 1.0, 0.0)
    within = dot(day2.astype(BF16), upper.astype(BF16))
    place = []
    offset = jnp.zeros((1, 1), F32)
    for r in range(rows):
        place.append(within[r : r + 1] + offset)
        offset = offset + within[r : r + 1, LANES - 1 :]
    order = jnp.where(day > 0.0, jnp.concatenate(place, 1) - 1.0, -1.0).astype(jnp.int32)
    count = jnp.sum(day).astype(jnp.int32)
    chunks = (count + CHUNK - 1) // CHUNK
    blocks = (count + HALF - 1) // HALF

    out_s[...] = jnp.zeros_like(out_s)
    fin_s[...] = jnp.zeros_like(fin_s)

    def gather(c, _):
        start = pl.multiple_of(c * CHUNK, CHUNK)
        hot = jnp.where(iota((CHUNK, columns), 0) + start == order, 1.0, 0.0).astype(BF16)
        pick_s[pl.ds(start, CHUNK), :] = hot
        out = dot(pred_s[...], hot, ((1,), (1,)))
        for j in range(CHUNK // LANES):
            piece = out[:, j * LANES : (j + 1) * LANES]
            at = c * (CHUNK // LANES) + j
            gather_s[at, pl.ds(0, base), :] = piece[:base]
            for r, k in enumerate((0, 0, 0, 1, 1, 2)):
                gather_s[at, pl.ds(base + r * levels, levels), :] = piece[
                    base + k * levels : base + (k + 1) * levels
                ]
            gather_s[at, pl.ds(base + 6 * levels, 2 * levels), :] = jnp.zeros(
                (2 * levels, LANES), F32
            )
            gather_s[at, pl.ds(gtail, 8), :] = piece[tail : tail + 8]
        return 0

    lax.fori_loop(0, chunks, gather, 0)

    lane_low = iota((1, LANES), 1) < HALF
    part = grows // 2

    def fold(x):
        return jnp.sum(x.reshape(x.shape[0] // 8, 8, LANES), 0)

    def block(b, _):
        chunk = b // 2
        odd = b % 2
        shift = HALF * odd

        def duplicate(x):
            return jnp.where(
                lane_low, pltpu.roll(x, shift, 1), pltpu.roll(x, HALF - shift, 1)
            )

        def tau_level(l, _):
            x = duplicate(gather_s[chunk, pl.ds(l, npred + 8, stride=levels), :])
            x = jnp.concatenate([jnp.where(lane_low, x, 0.0), jnp.where(lane_low, 0.0, x)], 0)
            tau_s[l] = dot(lhs_ref[...], x.astype(BF16))
            return 0

        lax.fori_loop(0, levels, tau_level, 0, unroll=4)

        ex = duplicate(gather_s[chunk, pl.ds(gtail, 8), :])
        cosine = ex[0:1] + ex[1:2] + ex[2:3]
        albedo = ex[3:4] + ex[4:5] + ex[5:6]
        slope = -LOG2E / cosine
        mass = duplicate(
            gather_s[chunk, pl.ds(base, levels), :]
            + gather_s[chunk, pl.ds(base + 3 * levels, levels), :]
            + gather_s[chunk, pl.ds(base + 5 * levels, levels), :]
        )
        mass_s[...] = mass
        net_s[...] = jnp.zeros_like(net_s)

        def group_of(gi, _):
            gs = pl.ds(pl.multiple_of(gi * part, 8), part)

            def down(l, carry):
                back, emit, direct = carry
                net_s[l] += fold(direct + emit)
                tau = tau_s[l, gs, :]
                ext = jnp.exp2(tau * (-DIFFUSIVITY * LOG2E))
                beam = jnp.exp2(tau * slope)
                half_w = rayh_ref[gs, :] * mass_s[pl.ds(l, 1), :] * pl.reciprocal(tau)
                reflect = half_w * (1.0 - ext)
                transmit = ext + reflect
                lower = direct * beam
                source = half_w * (direct - lower)
                inv = pl.reciprocal(1.0 - reflect * back)
                trans = transmit * inv
                trans_s[l, gs, :] = trans
                emit_s[l, gs, :] = (source + reflect * emit) * inv
                back_s[l, gs, :] = back
                new_back = reflect + (transmit * back) * trans
                new_emit = source + trans * (emit + back * source)
                return new_back, new_emit, lower

            zero = jnp.zeros((part, LANES), F32)
            back, emit, direct = lax.fori_loop(
                0, levels, down, (zero, zero, sun_ref[gs, :] * cosine), unroll=2
            )
            up = albedo * (emit + direct) * pl.reciprocal(1.0 - albedo * back)
            dif = emit + back * up
            sfc_s[gi, 0] = fold(direct)
            sfc_s[gi, 1] = fold(dif)
            net_s[levels] += fold(direct + dif - up)

            def rise(j, up):
                l = levels - 1 - j
                up = trans_s[l, gs, :] * up + emit_s[l, gs, :]
                net_s[l] -= fold(up - back_s[l, gs, :] * up)
                return up

            up = lax.fori_loop(0, levels, rise, up, unroll=2)
            sfc_s[gi, 2] = fold(up)
            return 0

        lax.fori_loop(0, 2, group_of, 0)

        net = jnp.sum(net_s[...], 1)
        heat = HEAT_FACTOR * (net[:levels] - net[1:])
        sfc = jnp.sum(sfc_s[0] + sfc_s[1], 1)
        out = jnp.concatenate([heat, sfc, jnp.zeros((5, LANES), F32)], 0)
        out = out + pltpu.roll(out, HALF, 1)
        out = out / jnp.concatenate([mass, jnp.ones((8, LANES), F32)], 0)
        valid = iota((1, LANES), 1) % HALF + b * HALF < count
        mine = iota((1, LANES), 1) // HALF == odd
        out_s[chunk] = jnp.where(mine, jnp.where(valid, out, 0.0), out_s[chunk])
        return 0

    lax.fori_loop(0, blocks, block, 0)

    def spread(c, _):
        two = jnp.concatenate([out_s[(CHUNK // LANES) * c + j] for j in range(CHUNK // LANES)], 1)
        rows = two.shape[0]
        back = dot(
            jnp.concatenate([x.astype(F32) for x in split3(two)], 0).astype(BF16),
            pick_s[pl.ds(pl.multiple_of(c * CHUNK, CHUNK), CHUNK), :],
        )
        fin_s[...] += back[:rows] + back[rows : 2 * rows] + back[2 * rows :]
        return 0

    lax.fori_loop(0, chunks, spread, 0)

    heat_ref[...] = fin_s[pl.ds(0, levels), :]
    sfc = fin_s[pl.ds(levels, 8), :]
    vals = jnp.concatenate([jnp.where(slot_hot, sfc[q : q + 1], 0.0) for q in range(3)], 0)
    hot = owner_hot()
    send = sum(dot(hot, x, ((1,), (1,))) for x in split3(vals))
    send_ref[...] = jnp.concatenate([send, jnp.zeros((devices, LANES - 3 * per), F32)], 1)


def recv_kernel(recv_ref, out_ref):
    devices = recv_ref.shape[0]
    width = out_ref.shape[1]
    per = width // devices
    group = LANES // per
    lane = iota((LANES, 3 * LANES), 1)
    hot = jnp.where(iota((LANES, 3 * LANES), 0) == lane // LANES * per + lane % per, 1.0, 0.0)
    hot = hot.astype(BF16)
    x = sum(dot(term, hot) for term in split3(recv_ref[...]))
    shape = (devices, 3 * LANES)
    x = jnp.where(iota(shape, 1) % LANES // per == iota(shape, 0) % group, x, 0.0)
    x = jnp.sum(x.reshape(devices // group, group, 3 * LANES), 1)
    for q in range(3):
        for r in range(devices // group):
            out_ref[q : q + 1, r * LANES : (r + 1) * LANES] = x[
                r : r + 1, q * LANES : (q + 1) * LANES
            ]


def exchange(x):
    rows = x.shape[0]
    y = lax.all_to_all(
        x.reshape(rows, 1, LANES), AXES, split_axis=0, concat_axis=0, tiled=True
    )
    return y.reshape(rows, LANES)


def local(state, kdist, rayleigh, solar, span_map, cos_zenith, day_flag, albedo):
    fields, levels, columns = state.shape
    devices = lax.axis_size(AXES)
    per = columns // devices
    group = LANES // per
    rows = columns // LANES
    npred = kdist.shape[1]
    grows = kdist.shape[0] // 2

    sent = pl.pallas_call(
        send_kernel,
        out_shape=jax.ShapeDtypeStruct((devices, LANES), F32),
        name="send",
    )(
        cos_zenith.reshape(rows, LANES),
        day_flag.reshape(rows, LANES),
        albedo.reshape(rows, LANES),
    )
    recv = exchange(sent)

    r1, r2, r3 = (x[:, None] for x in split3(rayleigh))
    zero = jnp.zeros_like(r1)
    terms = jnp.concatenate([kdist, r1, r2, r3, r1, r2, r1, zero, zero], 1)
    lhs = jnp.concatenate([terms[:grows], terms[grows:]], 1)

    def halves(x):
        return jnp.where(
            jnp.arange(LANES)[None, :] < HALF, x[:grows, None], x[grows:, None]
        )

    shift = (LANES - lax.axis_index(AXES) % group * per) % LANES
    chunks = columns // LANES
    g_array = pltpu.VMEM((levels, grows, LANES), F32)
    vmem = pl.BlockSpec(memory_space=pltpu.VMEM)
    heating, back = pl.pallas_call(
        main_kernel,
        out_shape=(
            jax.ShapeDtypeStruct((levels, columns), F32),
            jax.ShapeDtypeStruct((devices, LANES), F32),
        ),
        in_specs=[pl.BlockSpec(memory_space=pltpu.SMEM)] + [vmem] * 6,
        out_specs=(vmem, vmem),
        scratch_shapes=[
            pltpu.VMEM(((npred + 3) * levels + 16, columns), BF16),
            pltpu.VMEM((chunks, (npred + 8) * levels + 8, LANES), F32),
            pltpu.VMEM((columns, columns), BF16),
            g_array,
            g_array,
            g_array,
            g_array,
            pltpu.VMEM((levels + 1, 8, LANES), F32),
            pltpu.VMEM((2, 3, 8, LANES), F32),
            pltpu.VMEM((levels, LANES), F32),
            pltpu.VMEM((chunks, levels + 8, LANES), F32),
            pltpu.VMEM((levels + 8, columns), F32),
        ],
        compiler_params=pltpu.CompilerParams(vmem_limit_bytes=48 << 20),
        name="physics",
    )(
        shift.reshape(1).astype(jnp.int32),
        state,
        recv,
        span_map.reshape(1, columns),
        lhs,
        halves(0.5 * rayleigh),
        halves(solar),
    )
    surface = pl.pallas_call(
        recv_kernel,
        out_shape=jax.ShapeDtypeStruct((3, columns), F32),
        name="receive",
    )(exchange(back))
    return heating, surface


def solution(mesh):
    cols = P(AXES)
    in_specs = (P(None, None, AXES), P(), P(), P(), cols, cols, cols, cols)
    out_specs = (P(None, AXES), P(None, AXES))
    return jax.shard_map(
        local, mesh=mesh, in_specs=in_specs, out_specs=out_specs, check_vma=False
    )
```

```python
import jax
import jax.numpy as jnp
from jax import lax
from jax.experimental import pallas as pl
from jax.experimental.pallas import tpu as pltpu
from jax.sharding import PartitionSpec as P

AXES = ("gx", "gy")
F32 = jnp.float32
BF16 = jnp.bfloat16
LOG2E = 1.4426950408889634
DIFFUSIVITY = 1.66
HEAT_FACTOR = 8.0
LANES = 128
HALF = 64
UNROLL_DOWN = 8
UNROLL_RISE = 8
UNROLL_TAU = 8
CHUNK = 256


def split3(x):
    hi = x.astype(BF16)
    rest = x - hi.astype(F32)
    mid = rest.astype(BF16)
    low = (rest - mid.astype(F32)).astype(BF16)
    return hi, mid, low


def dot(a, b, dims=((1,), (0,))):
    return lax.dot_general(a, b, (dims, ((), ())), preferred_element_type=F32)


def iota(shape, dim):
    return lax.broadcasted_iota(jnp.int32, shape, dim)


def fetch(pairs, sems):
    copies = [pltpu.make_async_copy(a, b, sems.at[i]) for i, (a, b) in enumerate(pairs)]
    for c in copies:
        c.start()
    for c in copies:
        c.wait()


def send_kernel(cos_hbm, day_hbm, alb_hbm, out_ref, cos_ref, day_ref, alb_ref, sems):
    fetch(((cos_hbm, cos_ref), (day_hbm, day_ref), (alb_hbm, alb_ref)), sems)
    rows = cos_ref.shape[0]
    devices = out_ref.shape[0]
    group = devices // rows
    per = LANES // group
    keep = iota((devices, LANES), 1) // per == iota((devices, LANES), 0) % group
    cosine = jnp.where(day_ref[...] == 1, cos_ref[...], 0.0)

    def spread(x):
        x = jnp.broadcast_to(x[:, None, :], (rows, group, LANES)).reshape(devices, LANES)
        return jnp.where(keep, x, 0.0)

    out_ref[...] = spread(cosine) + pltpu.roll(spread(alb_ref[...]), per, 1)


def predictor_kernel(
    state_hbm,
    kdist_hbm,
    ray_hbm,
    solar_hbm,
    span_hbm,
    out_ref,
    lhs_ref,
    rayh_ref,
    sun_ref,
    owner_ref,
    slot_ref,
    state_ref,
    kdist_ref,
    ray_ref,
    solar_ref,
    span_ref,
    sems,
):
    pairs = (
        (kdist_hbm, kdist_ref),
        (ray_hbm, ray_ref),
        (solar_hbm, solar_ref),
        (span_hbm, span_ref),
        (state_hbm, state_ref),
    )
    fetch(pairs, sems)
    fields, levels, columns = state_ref.shape
    gases = fields - 2
    devices = owner_ref.shape[0]
    span = span_ref[...]
    hot = jnp.where(iota((devices, columns), 0) == span // columns, 1.0, 0.0)
    owner_ref[...] = hot.astype(BF16)
    slot_ref[...] = span % (columns // devices)

    def level(l, _):
        t = state_ref[0, pl.ds(l, 1), :] / 250.0
        m = state_ref[1, pl.ds(l, 1), :]
        q = jnp.concatenate([state_ref[2 + i, pl.ds(l, 1), :] for i in range(gases)], 0)
        modes = (None, t, t * t, 1.0 / t)
        v = [(q if b == 0 else q * modes[b]) * m for b in range(4)]
        at = pl.multiple_of(l * 4 * gases, 4 * gases)
        out_ref[pl.ds(at, 4 * gases), :] = jnp.concatenate(v, 0).astype(BF16)
        return 0

    lax.fori_loop(0, levels, level, 0, unroll=2)
    base = 4 * gases * levels
    for j, term in enumerate(split3(state_ref[1])):
        out_ref[pl.ds(base + j * levels, levels), :] = term

    npred, points = kdist_ref.shape
    rows = points // 2
    lane_low = iota((1, LANES), 1) < HALF
    source, target = iota((npred, npred), 0), iota((npred, npred), 1)
    move = jnp.where(source == target % gases * 4 + target // gases, 1.0, 0.0).astype(BF16)
    scale = -DIFFUSIVITY * LOG2E
    k1, k2, _ = split3(scale * dot(kdist_ref[...], move, ((0,), (0,))))

    def column(ref):
        return jnp.broadcast_to(ref[...], (LANES, points)).T

    ray = scale * column(ray_ref)
    r1, r2, r3 = (x.astype(F32)[:, :16] for x in split3(ray))
    place = iota((points, 16), 1)
    r = jnp.where(place == 2, r3, 0.0)
    r = jnp.where(jnp.logical_or(place == 1, place == 4), r2, r)
    r = jnp.where(jnp.logical_or(jnp.logical_or(place == 0, place == 3), place == 5), r1, r)
    terms = jnp.concatenate([k1.astype(F32), k2.astype(F32), r], 1)
    low, high = terms[:rows], terms[rows:]
    none = jnp.zeros_like(low)
    for k, pair in enumerate(((low, none), (high, none), (low, high))):
        lhs_ref[k] = jnp.concatenate(pair, 1).astype(BF16)

    for x, ref in ((0.5 * ray, rayh_ref), (column(solar_ref), sun_ref)):
        low, high = x[:rows], x[rows:]
        for k, y in enumerate((low, high, jnp.where(lane_low, low, high))):
            ref[2 * k] = y[: rows // 2]
            ref[2 * k + 1] = y[rows // 2 :]


def main_kernel(
    shift_ref,
    pred_ref,
    recv_ref,
    owner_ref,
    slot_ref,
    lhs_ref,
    rayh_ref,
    sun_ref,
    heat_ref,
    send_ref,
    extra_s,
    mass_s,
    pick_s,
    rhs_s,
    aux_s,
    tau0_s,
    tau1_s,
    trans_s,
    emit_s,
    back_s,
    net_s,
    sfc_s,
    out_s,
    fin_s,
):
    levels = heat_ref.shape[0]
    columns = pred_ref.shape[1]
    npred = pred_ref.shape[0] // levels - 3
    devices = recv_ref.shape[0]
    per = columns // devices
    part = rayh_ref.shape[1]
    base = npred * levels
    lane_low = iota((1, LANES), 1) < HALF
    half_rows = rhs_s.shape[2] // 2
    tau_s = (tau0_s, tau1_s)

    slot_hot = iota((per, columns), 0) == slot_ref[...]
    recv = pltpu.roll(recv_ref[...], shift_ref[0], 1).T[: 2 * per]
    sel = dot(jnp.concatenate(split3(recv), 0), owner_ref[...])
    sel = sel[: 2 * per] + sel[2 * per : 4 * per] + sel[4 * per :]
    cos_e = jnp.sum(jnp.where(slot_hot, sel[:per], 0.0), 0, keepdims=True)
    alb_e = jnp.sum(jnp.where(slot_hot, sel[per:], 0.0), 0, keepdims=True)
    extra = [x.astype(F32) for x in (*split3(cos_e), *split3(alb_e))]
    extra = jnp.concatenate(extra + [jnp.zeros((10, columns), F32)], 0)
    extra_s[...] = extra.astype(BF16)

    day = jnp.where(cos_e > 0.0, 1.0, 0.0)
    rows = columns // LANES
    day2 = jnp.concatenate([day[:, r * LANES : (r + 1) * LANES] for r in range(rows)], 0)
    upper = jnp.where(iota((LANES, LANES), 0) <= iota((LANES, LANES), 1), 1.0, 0.0)
    within = dot(day2.astype(BF16), upper.astype(BF16))
    place = []
    offset = jnp.zeros((1, 1), F32)
    for r in range(rows):
        place.append(within[r : r + 1] + offset)
        offset = offset + within[r : r + 1, LANES - 1 :]
    order = jnp.where(day > 0.0, jnp.concatenate(place, 1) - 1.0, -1.0).astype(jnp.int32)
    count = jnp.sum(day).astype(jnp.int32)
    chunks = (count + CHUNK - 1) // CHUNK
    units = (count + HALF - 1) // HALF

    def is_tail(unit):
        return jnp.logical_and(unit == units - 1, unit % 2 == 0)

    out_s[...] = jnp.zeros_like(out_s)
    fin_s[...] = jnp.zeros_like(fin_s)

    def gather(c, _):
        start = pl.multiple_of(c * CHUNK, CHUNK)
        hot = jnp.where(iota((CHUNK, columns), 0) + start == order, 1.0, 0.0).astype(BF16)
        pick_s[pl.ds(start, CHUNK), :] = hot
        out = dot(pred_ref[...], hot, ((1,), (1,)))
        more = dot(extra_s[...], hot, ((1,), (1,)))
        sub = iota((16, LANES), 0)
        for j in range(CHUNK // LANES):
            chunk = c * (CHUNK // LANES) + j
            piece = out[:, j * LANES : (j + 1) * LANES]
            ms = [piece[base + k * levels : base + (k + 1) * levels] for k in range(3)]
            for k in range(3):
                mass_s[k] = ms[k]
            ex = more[:8, j * LANES : (j + 1) * LANES]
            cosine = ex[0:1] + ex[1:2] + ex[2:3]
            albedo = ex[3:4] + ex[4:5] + ex[5:6]
            aux = jnp.concatenate(
                [ms[0] + ms[1] + ms[2], cosine, albedo, jnp.ones((6, LANES), F32)], 0
            )
            tail = is_tail(2 * chunk)
            aux_s[chunk] = jnp.where(
                jnp.logical_or(lane_low, jnp.logical_not(tail)), aux, pltpu.roll(aux, HALF, 1)
            )
            for l in range(levels):
                x = piece[l * npred : (l + 1) * npred].astype(BF16)
                rows = [mass_s[k, pl.ds(l, 1), :] for k in range(3)]
                y = jnp.where(sub < 3, rows[0], jnp.where(sub < 5, rows[1], rows[2]))
                y = jnp.where(sub < 6, y, 0.0).astype(BF16)
                at = pl.ds(l % 2 * LANES, LANES)
                rhs_s[chunk, l // 2, pl.ds(0, npred), at] = x
                rhs_s[chunk, l // 2, pl.ds(npred, npred), at] = x
                rhs_s[chunk, l // 2, pl.ds(2 * npred, 16), at] = y
                rhs_s[chunk, l // 2, pl.ds(half_rows, half_rows), at] = jnp.zeros(
                    (half_rows, LANES), BF16
                )

            @pl.when(tail)
            def _():
                def pair(l, _):
                    for j in range(2):
                        at = pl.ds(j * LANES, LANES)
                        x = rhs_s[chunk, l, pl.ds(0, half_rows), at].astype(F32)
                        low = jnp.where(lane_low, x, 0.0)
                        high = pltpu.roll(low, HALF, 1)
                        rhs_s[chunk, l, :, at] = jnp.concatenate([low, high], 0).astype(BF16)
                    return 0

                lax.fori_loop(0, levels // 2, pair, 0, unroll=2)

        return 0

    lax.fori_loop(0, chunks, gather, 0)

    def fold(x):
        return jnp.sum(x.reshape(x.shape[0] // 8, 8, LANES), 0)

    def where_is(unit):
        kind = jnp.where(is_tail(unit), 2, unit % 2)
        return unit // 2, kind

    def one(unit, slot):
        chunk, kind = where_is(unit)
        g = 2 * kind + slot
        now = tau_s[slot]
        cosine = aux_s[chunk, pl.ds(levels, 1), :]
        albedo = aux_s[chunk, pl.ds(levels + 1, 1), :]
        slope = 1.0 / (DIFFUSIVITY * cosine)

        if slot == 0:

            def optical(l, _):
                out = dot(lhs_ref[kind], rhs_s[chunk, l])
                for s in range(2):
                    for j in range(2):
                        tau_s[s][2 * l + j] = out[s * part : (s + 1) * part, j * LANES : (j + 1) * LANES]
                return 0

            lax.fori_loop(0, levels // 2, optical, 0, unroll=UNROLL_TAU)

            @pl.when(kind != 1)
            def _():
                net_s[...] = jnp.zeros_like(net_s)
                sfc_s[...] = jnp.zeros_like(sfc_s)

        def down(l, carry):
            back, emit, direct = carry
            net_s[l] += fold(direct + emit)
            tau = now[l]
            ext = jnp.exp2(tau)
            beam = jnp.exp2(tau * slope)
            half_w = rayh_ref[g] * aux_s[chunk, pl.ds(l, 1), :] * pl.reciprocal(tau)
            reflect = half_w * (1.0 - ext)
            transmit = ext + reflect
            lower = direct * beam
            source = half_w * (direct - lower)
            inv = pl.reciprocal(1.0 - reflect * back)
            trans = transmit * inv
            trans_s[l] = trans
            emit_s[l] = (source + reflect * emit) * inv
            back_s[l] = back
            new_back = reflect + (transmit * back) * trans
            new_emit = source + trans * (emit + back * source)
            return new_back, new_emit, lower

        zero = jnp.zeros((part, LANES), F32)
        back, emit, direct = lax.fori_loop(
            0, levels, down, (zero, zero, sun_ref[g] * cosine), unroll=UNROLL_DOWN
        )
        up = albedo * (emit + direct) * pl.reciprocal(1.0 - albedo * back)
        dif = emit + back * up
        sfc_s[0] += fold(direct)
        sfc_s[1] += fold(dif)
        net_s[levels] += fold(direct + dif - up)

        def rise(j, up):
            l = levels - 1 - j
            up = trans_s[l] * up + emit_s[l]
            net_s[l] -= fold(up - back_s[l] * up)
            return up

        up = lax.fori_loop(0, levels, rise, up, unroll=UNROLL_RISE)
        sfc_s[2] += fold(up)

        if slot == 0:
            return

        @pl.when(kind != 0)
        def _():
            net = jnp.sum(net_s[...], 1)
            heat = HEAT_FACTOR * (net[:levels] - net[1:])
            out = jnp.concatenate([heat, jnp.sum(sfc_s[...], 1), jnp.zeros((5, LANES), F32)], 0)
            out = jnp.where(kind == 2, out + pltpu.roll(out, HALF, 1), out)
            mass = aux_s[chunk, pl.ds(0, levels), :]
            out = out / jnp.concatenate([mass, jnp.ones((8, LANES), F32)], 0)
            out_s[chunk] = jnp.where(iota((1, LANES), 1) + chunk * LANES < count, out, 0.0)

    def both(unit, _):
        one(unit, 0)
        one(unit, 1)
        return 0

    lax.fori_loop(0, units, both, 0)

    def spread(c, _):
        two = jnp.concatenate([out_s[(CHUNK // LANES) * c + j] for j in range(CHUNK // LANES)], 1)
        rows = two.shape[0]
        back = dot(
            jnp.concatenate([x.astype(F32) for x in split3(two)], 0).astype(BF16),
            pick_s[pl.ds(pl.multiple_of(c * CHUNK, CHUNK), CHUNK), :],
        )
        fin_s[...] += back[:rows] + back[rows : 2 * rows] + back[2 * rows :]
        return 0

    lax.fori_loop(0, chunks, spread, 0)

    heat_ref[...] = fin_s[pl.ds(0, levels), :]
    sfc = fin_s[pl.ds(levels, 8), :]
    vals = jnp.concatenate([jnp.where(slot_hot, sfc[q : q + 1], 0.0) for q in range(3)], 0)
    hot = owner_ref[...]
    send = sum(dot(hot, x, ((1,), (1,))) for x in split3(vals))
    send_ref[...] = jnp.concatenate([send, jnp.zeros((devices, LANES - 3 * per), F32)], 1)


def recv_kernel(recv_ref, out_ref):
    devices = recv_ref.shape[0]
    width = out_ref.shape[1]
    per = width // devices
    group = LANES // per
    lane = iota((LANES, 3 * LANES), 1)
    hot = jnp.where(iota((LANES, 3 * LANES), 0) == lane // LANES * per + lane % per, 1.0, 0.0)
    hot = hot.astype(BF16)
    x = sum(dot(term, hot) for term in split3(recv_ref[...]))
    shape = (devices, 3 * LANES)
    x = jnp.where(iota(shape, 1) % LANES // per == iota(shape, 0) % group, x, 0.0)
    x = jnp.sum(x.reshape(devices // group, group, 3 * LANES), 1)
    for q in range(3):
        for r in range(devices // group):
            out_ref[q : q + 1, r * LANES : (r + 1) * LANES] = x[
                r : r + 1, q * LANES : (q + 1) * LANES
            ]


def exchange(x):
    rows = x.shape[0]
    y = lax.all_to_all(
        x.reshape(rows, 1, LANES), AXES, split_axis=0, concat_axis=0, tiled=True
    )
    return y.reshape(rows, LANES)


def in_hbm(x):
    return pltpu.with_memory_space_constraint(x, pltpu.HBM)


def local(state, kdist, rayleigh, solar, span_map, cos_zenith, day_flag, albedo):
    fields, levels, columns = state.shape
    devices = lax.axis_size(AXES)
    per = columns // devices
    group = LANES // per
    rows = columns // LANES
    npred = kdist.shape[1]
    grows = kdist.shape[0] // 2

    hbm = pl.BlockSpec(memory_space=pltpu.HBM)
    sent = pl.pallas_call(
        send_kernel,
        out_shape=jax.ShapeDtypeStruct((devices, LANES), F32),
        in_specs=[hbm] * 3,
        scratch_shapes=[
            pltpu.VMEM((rows, LANES), F32),
            pltpu.VMEM((rows, LANES), jnp.int32),
            pltpu.VMEM((rows, LANES), F32),
            pltpu.SemaphoreType.DMA((3,)),
        ],
        compiler_params=pltpu.CompilerParams(vmem_limit_bytes=4 << 20),
        name="send",
    )(
        in_hbm(cos_zenith.reshape(rows, LANES)),
        in_hbm(day_flag.reshape(rows, LANES)),
        in_hbm(albedo.reshape(rows, LANES)),
    )
    recv = exchange(sent)
    points = 2 * grows
    preds, lhs, rayh, sun, owner, slot = pl.pallas_call(
        predictor_kernel,
        out_shape=(
            jax.ShapeDtypeStruct(((npred + 3) * levels, columns), BF16),
            jax.ShapeDtypeStruct((3, grows, 4 * npred + 32), BF16),
            jax.ShapeDtypeStruct((6, grows // 2, LANES), F32),
            jax.ShapeDtypeStruct((6, grows // 2, LANES), F32),
            jax.ShapeDtypeStruct((devices, columns), BF16),
            jax.ShapeDtypeStruct((1, columns), jnp.int32),
        ),
        in_specs=[hbm] * 5,
        scratch_shapes=[
            pltpu.VMEM((fields, levels, columns), F32),
            pltpu.VMEM((npred, points), BF16),
            pltpu.VMEM((1, points), F32),
            pltpu.VMEM((1, points), F32),
            pltpu.VMEM((1, columns), jnp.int32),
            pltpu.SemaphoreType.DMA((5,)),
        ],
        compiler_params=pltpu.CompilerParams(vmem_limit_bytes=12 << 20),
        name="predictors",
    )(
        in_hbm(state),
        in_hbm(kdist.T),
        in_hbm(rayleigh.reshape(1, -1)),
        in_hbm(solar.reshape(1, -1)),
        in_hbm(span_map.reshape(1, columns)),
    )
    shift = (LANES - lax.axis_index(AXES) % group * per) % LANES
    chunks = columns // LANES
    g_array = pltpu.VMEM((levels, grows // 2, LANES), F32)
    vmem = pl.BlockSpec(memory_space=pltpu.VMEM)
    heating, back = pl.pallas_call(
        main_kernel,
        out_shape=(
            jax.ShapeDtypeStruct((levels, columns), F32),
            jax.ShapeDtypeStruct((devices, LANES), F32),
        ),
        in_specs=[pl.BlockSpec(memory_space=pltpu.SMEM)] + [vmem] * 7,
        out_specs=(vmem, vmem),
        scratch_shapes=[
            pltpu.VMEM((16, columns), BF16),
            pltpu.VMEM((3, levels, LANES), F32),
            pltpu.VMEM((columns, columns), BF16),
            pltpu.VMEM((chunks, levels // 2, lhs.shape[2], 2 * LANES), BF16),
            pltpu.VMEM((chunks, levels + 8, LANES), F32),
            g_array,
            g_array,
            g_array,
            g_array,
            g_array,
            pltpu.VMEM((levels + 1, 8, LANES), F32),
            pltpu.VMEM((3, 8, LANES), F32),
            pltpu.VMEM((chunks, levels + 8, LANES), F32),
            pltpu.VMEM((levels + 8, columns), F32),
        ],
        compiler_params=pltpu.CompilerParams(vmem_limit_bytes=26 << 20),
        name="physics",
    )(
        shift.reshape(1).astype(jnp.int32),
        preds,
        recv,
        owner,
        slot,
        lhs,
        rayh,
        sun,
    )
    surface = pl.pallas_call(
        recv_kernel,
        out_shape=jax.ShapeDtypeStruct((3, columns), F32),
        compiler_params=pltpu.CompilerParams(vmem_limit_bytes=4 << 20),
        name="receive",
    )(exchange(back))
    return heating, surface


def solution(mesh):
    cols = P(AXES)
    in_specs = (P(None, None, AXES), P(), P(), P(), cols, cols, cols, cols)
    out_specs = (P(None, AXES), P(None, AXES))
    return jax.shard_map(
        local, mesh=mesh, in_specs=in_specs, out_specs=out_specs, check_vma=False
    )
```

```python
import jax
import jax.numpy as jnp
from jax import lax
from jax.experimental import pallas as pl
from jax.experimental.pallas import tpu as pltpu
from jax.sharding import PartitionSpec as P

AXES = ("gx", "gy")
F32 = jnp.float32
BF16 = jnp.bfloat16
LOG2E = 1.4426950408889634
DIFFUSIVITY = 1.66
HEAT_FACTOR = 8.0
LANES = 128
HALF = 64
UNROLL_DOWN = 16
UNROLL_RISE = 32
UNROLL_TAU = 8
CHUNK = 256


def split3(x):
    hi = x.astype(BF16)
    rest = x - hi.astype(F32)
    mid = rest.astype(BF16)
    low = (rest - mid.astype(F32)).astype(BF16)
    return hi, mid, low


def dot(a, b, dims=((1,), (0,))):
    return lax.dot_general(a, b, (dims, ((), ())), preferred_element_type=F32)


def iota(shape, dim):
    return lax.broadcasted_iota(jnp.int32, shape, dim)


def fetch(pairs, sems):
    copies = [pltpu.make_async_copy(a, b, sems.at[i]) for i, (a, b) in enumerate(pairs)]
    for c in copies:
        c.start()
    for c in copies:
        c.wait()


def send_kernel(cos_hbm, day_hbm, alb_hbm, out_ref, cos_ref, day_ref, alb_ref, sems):
    fetch(((cos_hbm, cos_ref), (day_hbm, day_ref), (alb_hbm, alb_ref)), sems)
    rows = cos_ref.shape[0]
    devices = out_ref.shape[0]
    group = devices // rows
    per = LANES // group
    keep = iota((devices, LANES), 1) // per == iota((devices, LANES), 0) % group
    cosine = jnp.where(day_ref[...] == 1, cos_ref[...], 0.0)

    def spread(x):
        x = jnp.broadcast_to(x[:, None, :], (rows, group, LANES)).reshape(devices, LANES)
        return jnp.where(keep, x, 0.0)

    out_ref[...] = spread(cosine) + pltpu.roll(spread(alb_ref[...]), per, 1)


def predictor_kernel(
    state_hbm,
    kdist_hbm,
    ray_hbm,
    solar_hbm,
    span_hbm,
    out_ref,
    lhs_ref,
    tail_ref,
    rayh_ref,
    sun_ref,
    owner_ref,
    slot_ref,
    state_ref,
    kdist_ref,
    ray_ref,
    solar_ref,
    span_ref,
    sems,
):
    pairs = (
        (kdist_hbm, kdist_ref),
        (ray_hbm, ray_ref),
        (solar_hbm, solar_ref),
        (span_hbm, span_ref),
        (state_hbm, state_ref),
    )
    fetch(pairs, sems)
    fields, levels, columns = state_ref.shape
    gases = fields - 2
    devices = owner_ref.shape[0]
    span = span_ref[...]
    hot = jnp.where(iota((devices, columns), 0) == span // columns, 1.0, 0.0)
    owner_ref[...] = hot.astype(BF16)
    slot_ref[...] = span % (columns // devices)

    def level(l, _):
        t = state_ref[0, pl.ds(l, 1), :] / 250.0
        m = state_ref[1, pl.ds(l, 1), :]
        q = jnp.concatenate([state_ref[2 + i, pl.ds(l, 1), :] for i in range(gases)], 0)
        modes = (None, t, t * t, 1.0 / t)
        v = [(q if b == 0 else q * modes[b]) * m for b in range(4)]
        at = pl.multiple_of(l * 4 * gases, 4 * gases)
        out_ref[pl.ds(at, 4 * gases), :] = jnp.concatenate(v, 0).astype(BF16)
        return 0

    lax.fori_loop(0, levels, level, 0, unroll=2)
    base = 4 * gases * levels
    for j, term in enumerate(split3(state_ref[1])):
        out_ref[pl.ds(base + j * levels, levels), :] = term

    npred, points = kdist_ref.shape
    rows = points // 2
    lane_low = iota((1, LANES), 1) < HALF
    source, target = iota((npred, npred), 0), iota((npred, npred), 1)
    move = jnp.where(source == target % gases * 4 + target // gases, 1.0, 0.0).astype(BF16)
    scale = -DIFFUSIVITY * LOG2E
    k1, k2, _ = split3(scale * dot(kdist_ref[...], move, ((0,), (0,))))

    def column(ref):
        return jnp.broadcast_to(ref[...], (LANES, points)).T

    ray = scale * column(ray_ref)
    r1, r2, r3 = (x.astype(F32)[:, :16] for x in split3(ray))
    place = iota((points, 16), 1)
    r = jnp.where(place == 2, r3, 0.0)
    r = jnp.where(jnp.logical_or(place == 1, place == 4), r2, r)
    r = jnp.where(jnp.logical_or(jnp.logical_or(place == 0, place == 3), place == 5), r1, r)
    terms = jnp.concatenate([k1.astype(F32), k2.astype(F32), r], 1)
    low, high = terms[:rows], terms[rows:]
    lhs_ref[...] = terms.astype(BF16)
    tail_ref[...] = jnp.concatenate([low, high], 1).astype(BF16)

    for x, ref in ((0.5 * ray, rayh_ref), (column(solar_ref), sun_ref)):
        low, high = x[:rows], x[rows:]
        for k, y in enumerate((low, high, jnp.where(lane_low, low, high))):
            ref[2 * k] = y[: rows // 2]
            ref[2 * k + 1] = y[rows // 2 :]


def main_kernel(
    shift_ref,
    pred_ref,
    recv_ref,
    owner_ref,
    slot_ref,
    lhs_ref,
    tail_ref,
    rayh_ref,
    sun_ref,
    heat_ref,
    send_ref,
    extra_s,
    picked_s,
    mass_s,
    pick_s,
    rhs_s,
    aux_s,
    tau_s,
    half_s,
    trans_s,
    emit_s,
    back_s,
    net_s,
    sfc_s,
    out_s,
    fin_s,
):
    levels = heat_ref.shape[0]
    columns = pred_ref.shape[1]
    npred = pred_ref.shape[0] // levels - 3
    devices = recv_ref.shape[0]
    per = columns // devices
    part = rayh_ref.shape[1]
    base = npred * levels
    lane_low = iota((1, LANES), 1) < HALF
    half_rows = rhs_s.shape[2] // 2

    slot_hot = iota((per, columns), 0) == slot_ref[...]
    recv = pltpu.roll(recv_ref[...], shift_ref[0], 1).T[: 2 * per]
    sel = dot(jnp.concatenate(split3(recv), 0), owner_ref[...])
    sel = sel[: 2 * per] + sel[2 * per : 4 * per] + sel[4 * per :]
    cos_e = jnp.sum(jnp.where(slot_hot, sel[:per], 0.0), 0, keepdims=True)
    alb_e = jnp.sum(jnp.where(slot_hot, sel[per:], 0.0), 0, keepdims=True)
    extra = [x.astype(F32) for x in (*split3(cos_e), *split3(alb_e))]
    extra = jnp.concatenate(extra + [jnp.zeros((10, columns), F32)], 0)
    extra_s[...] = extra.astype(BF16)

    day = jnp.where(cos_e > 0.0, 1.0, 0.0)
    rows = columns // LANES
    day2 = jnp.concatenate([day[:, r * LANES : (r + 1) * LANES] for r in range(rows)], 0)
    upper = jnp.where(iota((LANES, LANES), 0) <= iota((LANES, LANES), 1), 1.0, 0.0)
    within = dot(day2.astype(BF16), upper.astype(BF16))
    place = []
    offset = jnp.zeros((1, 1), F32)
    for r in range(rows):
        place.append(within[r : r + 1] + offset)
        offset = offset + within[r : r + 1, LANES - 1 :]
    order = jnp.where(day > 0.0, jnp.concatenate(place, 1) - 1.0, -1.0).astype(jnp.int32)
    count = jnp.sum(day).astype(jnp.int32)
    before = [jnp.int32(0)]
    for k in range(columns // CHUNK):
        before.append(before[-1] + jnp.sum(day[:, k * CHUNK : (k + 1) * CHUNK]).astype(jnp.int32))
    chunks = (count + CHUNK - 1) // CHUNK
    units = (count + HALF - 1) // HALF

    def is_tail(unit):
        return jnp.logical_and(unit == units - 1, unit % 2 == 0)

    out_s[...] = jnp.zeros_like(out_s)
    fin_s[...] = jnp.zeros_like(fin_s)

    def gather(c, _):
        start = pl.multiple_of(c * CHUNK, CHUNK)
        hot = jnp.where(iota((CHUNK, columns), 0) + start == order, 1.0, 0.0).astype(BF16)
        pick_s[pl.ds(start, CHUNK), :] = hot
        for k in range(columns // CHUNK):
            at = slice(k * CHUNK, (k + 1) * CHUNK)

            def part_of():
                rows = jnp.concatenate([pred_ref[:, at], extra_s[:, at]], 0)
                return dot(rows, pick_s[pl.ds(start, CHUNK), at], ((1,), (1,)))

            @pl.when(jnp.logical_and(before[k] <= start, before[k + 1] > start))
            def _():
                picked_s[...] = part_of()

            @pl.when(jnp.logical_and(before[k] > start, before[k] < start + CHUNK))
            def _():
                picked_s[...] += part_of()

        sub = iota((16, LANES), 0)
        for j in range(CHUNK // LANES):
            chunk = c * (CHUNK // LANES) + j
            lanes = slice(j * LANES, (j + 1) * LANES)
            piece = picked_s.at[:, lanes]
            ms = [piece[base + k * levels : base + (k + 1) * levels, :] for k in range(3)]
            for k in range(3):
                mass_s[k] = ms[k]
            ex = piece[base + 3 * levels : base + 3 * levels + 8, :]
            cosine = ex[0:1] + ex[1:2] + ex[2:3]
            albedo = ex[3:4] + ex[4:5] + ex[5:6]
            aux = jnp.concatenate(
                [ms[0] + ms[1] + ms[2], cosine, albedo, jnp.ones((6, LANES), F32)], 0
            )
            tail = is_tail(2 * chunk)
            aux_s[chunk] = jnp.where(
                jnp.logical_or(lane_low, jnp.logical_not(tail)), aux, pltpu.roll(aux, HALF, 1)
            )
            for l in range(levels):
                x = piece[l * npred : (l + 1) * npred, :].astype(BF16)
                rows = [mass_s[k, pl.ds(l, 1), :] for k in range(3)]
                y = jnp.where(sub < 3, rows[0], jnp.where(sub < 5, rows[1], rows[2]))
                y = jnp.where(sub < 6, y, 0.0).astype(BF16)
                at = pl.ds(l % 2 * LANES, LANES)
                rhs_s[chunk, l // 2, pl.ds(0, npred), at] = x
                rhs_s[chunk, l // 2, pl.ds(npred, npred), at] = x
                rhs_s[chunk, l // 2, pl.ds(2 * npred, 16), at] = y

            @pl.when(tail)
            def _():
                def pair(l, _):
                    for j in range(2):
                        at = pl.ds(j * LANES, LANES)
                        x = rhs_s[chunk, l, pl.ds(npred, npred + 16), at].astype(F32)
                        x = pltpu.roll(x, HALF, 1).astype(BF16)
                        rhs_s[chunk, l, pl.ds(half_rows, npred), at] = x[:npred]
                        rhs_s[chunk, l, pl.ds(half_rows + npred, npred + 16), at] = x
                    return 0

                lax.fori_loop(0, levels // 2, pair, 0, unroll=2)

        return 0

    lax.fori_loop(0, chunks, gather, 0)

    def fold(x):
        return jnp.sum(x.reshape(x.shape[0] // 8, 8, LANES), 0)

    def where_is(unit):
        kind = jnp.where(is_tail(unit), 2, unit % 2)
        return unit // 2, kind

    def one(unit, slot):
        chunk, kind = where_is(unit)
        g = 2 * kind + slot
        now = tau_s.at[2 * (kind % 2) + slot]
        half = half_s.at[2 * (kind % 2) + slot]
        cosine = aux_s[chunk, pl.ds(levels, 1), :]
        albedo = aux_s[chunk, pl.ds(levels + 1, 1), :]
        slope = 1.0 / (DIFFUSIVITY * cosine)

        if slot == 0:

            def keep(l, out, first):
                for j in range(2):
                    mass = aux_s[chunk, pl.ds(2 * l + j, 1), :]
                    for s in range(out.shape[0] // part):
                        y = out[s * part : (s + 1) * part, j * LANES : (j + 1) * LANES]
                        tau_s[s, 2 * l + j] = y
                        half_s[s, 2 * l + j] = rayh_ref[first + s] * mass * pl.reciprocal(y)
                return 0

            @pl.when(kind == 0)
            def _():
                def pair(l, _):
                    return keep(l, dot(lhs_ref[...], rhs_s[chunk, l, :half_rows]), 0)

                lax.fori_loop(0, levels // 2, pair, 0, unroll=UNROLL_TAU)

            @pl.when(kind == 2)
            def _():
                def pair(l, _):
                    return keep(l, dot(tail_ref[...], rhs_s[chunk, l]), 4)

                lax.fori_loop(0, levels // 2, pair, 0, unroll=UNROLL_TAU)

            @pl.when(kind != 1)
            def _():
                net_s[...] = jnp.zeros_like(net_s)
                sfc_s[...] = jnp.zeros_like(sfc_s)

        def down(l, carry):
            back, emit, direct = carry
            net_s[l] += fold(direct + emit)
            tau = now[l]
            ext = jnp.exp2(tau)
            beam = jnp.exp2(tau * slope)
            half_w = half[l]
            reflect = half_w * (1.0 - ext)
            transmit = ext + reflect
            lower = direct * beam
            source = half_w * (direct - lower)
            inv = pl.reciprocal(1.0 - reflect * back)
            trans = transmit * inv
            trans_s[l] = trans
            emit_s[l] = (source + reflect * emit) * inv
            back_s[l] = back
            new_back = reflect + (transmit * back) * trans
            new_emit = source + trans * (emit + back * source)
            return new_back, new_emit, lower

        zero = jnp.zeros((part, LANES), F32)
        back, emit, direct = lax.fori_loop(
            0, levels, down, (zero, zero, sun_ref[g] * cosine), unroll=UNROLL_DOWN
        )
        up = albedo * (emit + direct) * pl.reciprocal(1.0 - albedo * back)
        dif = emit + back * up
        sfc_s[0] += fold(direct)
        sfc_s[1] += fold(dif)
        net_s[levels] += fold(direct + dif - up)

        def rise(j, up):
            l = levels - 1 - j
            up = trans_s[l] * up + emit_s[l]
            net_s[l] -= fold(up - back_s[l] * up)
            return up

        up = lax.fori_loop(0, levels, rise, up, unroll=UNROLL_RISE)
        sfc_s[2] += fold(up)

        if slot == 0:
            return

        @pl.when(kind != 0)
        def _():
            net = jnp.sum(net_s[...], 1)
            heat = HEAT_FACTOR * (net[:levels] - net[1:])
            out = jnp.concatenate([heat, jnp.sum(sfc_s[...], 1), jnp.zeros((5, LANES), F32)], 0)
            out = jnp.where(kind == 2, out + pltpu.roll(out, HALF, 1), out)
            mass = aux_s[chunk, pl.ds(0, levels), :]
            out = out / jnp.concatenate([mass, jnp.ones((8, LANES), F32)], 0)
            out_s[chunk] = jnp.where(iota((1, LANES), 1) + chunk * LANES < count, out, 0.0)

    def both(unit, _):
        one(unit, 0)
        one(unit, 1)
        return 0

    lax.fori_loop(0, units, both, 0)

    def spread(c, _):
        two = jnp.concatenate([out_s[(CHUNK // LANES) * c + j] for j in range(CHUNK // LANES)], 1)
        rows = two.shape[0]
        back = dot(
            jnp.concatenate([x.astype(F32) for x in split3(two)], 0).astype(BF16),
            pick_s[pl.ds(pl.multiple_of(c * CHUNK, CHUNK), CHUNK), :],
        )
        fin_s[...] += back[:rows] + back[rows : 2 * rows] + back[2 * rows :]
        return 0

    lax.fori_loop(0, chunks, spread, 0)

    heat_ref[...] = fin_s[pl.ds(0, levels), :]
    sfc = fin_s[pl.ds(levels, 8), :]
    vals = jnp.concatenate([jnp.where(slot_hot, sfc[q : q + 1], 0.0) for q in range(3)], 0)
    hot = owner_ref[...]
    send = sum(dot(hot, x, ((1,), (1,))) for x in split3(vals))
    send_ref[...] = jnp.concatenate([send, jnp.zeros((devices, LANES - 3 * per), F32)], 1)


def recv_kernel(recv_ref, out_ref):
    devices = recv_ref.shape[0]
    width = out_ref.shape[1]
    per = width // devices
    group = LANES // per
    lane = iota((LANES, 3 * LANES), 1)
    hot = jnp.where(iota((LANES, 3 * LANES), 0) == lane // LANES * per + lane % per, 1.0, 0.0)
    hot = hot.astype(BF16)
    x = sum(dot(term, hot) for term in split3(recv_ref[...]))
    shape = (devices, 3 * LANES)
    x = jnp.where(iota(shape, 1) % LANES // per == iota(shape, 0) % group, x, 0.0)
    x = jnp.sum(x.reshape(devices // group, group, 3 * LANES), 1)
    for q in range(3):
        for r in range(devices // group):
            out_ref[q : q + 1, r * LANES : (r + 1) * LANES] = x[
                r : r + 1, q * LANES : (q + 1) * LANES
            ]


def exchange(x):
    rows = x.shape[0]
    y = lax.all_to_all(
        x.reshape(rows, 1, LANES), AXES, split_axis=0, concat_axis=0, tiled=True
    )
    return y.reshape(rows, LANES)


def in_hbm(x):
    return pltpu.with_memory_space_constraint(x, pltpu.HBM)


def local(state, kdist, rayleigh, solar, span_map, cos_zenith, day_flag, albedo):
    fields, levels, columns = state.shape
    devices = lax.axis_size(AXES)
    per = columns // devices
    group = LANES // per
    rows = columns // LANES
    npred = kdist.shape[1]
    grows = kdist.shape[0] // 2

    hbm = pl.BlockSpec(memory_space=pltpu.HBM)
    sent = pl.pallas_call(
        send_kernel,
        out_shape=jax.ShapeDtypeStruct((devices, LANES), F32),
        in_specs=[hbm] * 3,
        scratch_shapes=[
            pltpu.VMEM((rows, LANES), F32),
            pltpu.VMEM((rows, LANES), jnp.int32),
            pltpu.VMEM((rows, LANES), F32),
            pltpu.SemaphoreType.DMA((3,)),
        ],
        compiler_params=pltpu.CompilerParams(vmem_limit_bytes=4 << 20),
        name="send",
    )(
        in_hbm(cos_zenith.reshape(rows, LANES)),
        in_hbm(day_flag.reshape(rows, LANES)),
        in_hbm(albedo.reshape(rows, LANES)),
    )
    recv = exchange(sent)
    points = 2 * grows
    preds, lhs, tail, rayh, sun, owner, slot = pl.pallas_call(
        predictor_kernel,
        out_shape=(
            jax.ShapeDtypeStruct(((npred + 3) * levels, columns), BF16),
            jax.ShapeDtypeStruct((points, 2 * npred + 16), BF16),
            jax.ShapeDtypeStruct((grows, 4 * npred + 32), BF16),
            jax.ShapeDtypeStruct((6, grows // 2, LANES), F32),
            jax.ShapeDtypeStruct((6, grows // 2, LANES), F32),
            jax.ShapeDtypeStruct((devices, columns), BF16),
            jax.ShapeDtypeStruct((1, columns), jnp.int32),
        ),
        in_specs=[hbm] * 5,
        scratch_shapes=[
            pltpu.VMEM((fields, levels, columns), F32),
            pltpu.VMEM((npred, points), BF16),
            pltpu.VMEM((1, points), F32),
            pltpu.VMEM((1, points), F32),
            pltpu.VMEM((1, columns), jnp.int32),
            pltpu.SemaphoreType.DMA((5,)),
        ],
        compiler_params=pltpu.CompilerParams(vmem_limit_bytes=12 << 20),
        name="predictors",
    )(
        in_hbm(state),
        in_hbm(kdist.T),
        in_hbm(rayleigh.reshape(1, -1)),
        in_hbm(solar.reshape(1, -1)),
        in_hbm(span_map.reshape(1, columns)),
    )
    shift = (LANES - lax.axis_index(AXES) % group * per) % LANES
    chunks = columns // LANES
    g_array = pltpu.VMEM((levels, grows // 2, LANES), F32)
    vmem = pl.BlockSpec(memory_space=pltpu.VMEM)
    heating, back = pl.pallas_call(
        main_kernel,
        out_shape=(
            jax.ShapeDtypeStruct((levels, columns), F32),
            jax.ShapeDtypeStruct((devices, LANES), F32),
        ),
        in_specs=[pl.BlockSpec(memory_space=pltpu.SMEM)] + [vmem] * 8,
        out_specs=(vmem, vmem),
        scratch_shapes=[
            pltpu.VMEM((16, columns), BF16),
            pltpu.VMEM(((npred + 3) * levels + 16, CHUNK), F32),
            pltpu.VMEM((3, levels, LANES), F32),
            pltpu.VMEM((columns, columns), BF16),
            pltpu.VMEM((chunks, levels // 2, tail.shape[1], 2 * LANES), BF16),
            pltpu.VMEM((chunks, levels + 8, LANES), F32),
            pltpu.VMEM((4, levels, grows // 2, LANES), F32),
            pltpu.VMEM((4, levels, grows // 2, LANES), F32),
            g_array,
            g_array,
            g_array,
            pltpu.VMEM((levels + 1, 8, LANES), F32),
            pltpu.VMEM((3, 8, LANES), F32),
            pltpu.VMEM((chunks, levels + 8, LANES), F32),
            pltpu.VMEM((levels + 8, columns), F32),
        ],
        compiler_params=pltpu.CompilerParams(vmem_limit_bytes=34 << 20),
        name="physics",
    )(
        shift.reshape(1).astype(jnp.int32),
        preds,
        recv,
        owner,
        slot,
        lhs,
        tail,
        rayh,
        sun,
    )
    surface = pl.pallas_call(
        recv_kernel,
        out_shape=jax.ShapeDtypeStruct((3, columns), F32),
        compiler_params=pltpu.CompilerParams(vmem_limit_bytes=4 << 20),
        name="receive",
    )(exchange(back))
    return heating, surface


def solution(mesh):
    cols = P(AXES)
    in_specs = (P(None, None, AXES), P(), P(), P(), cols, cols, cols, cols)
    out_specs = (P(None, AXES), P(None, AXES))
    return jax.shard_map(
        local, mesh=mesh, in_specs=in_specs, out_specs=out_specs, check_vma=False
    )
```

```python
import jax
import jax.numpy as jnp
from jax import lax
from jax.experimental import pallas as pl
from jax.experimental.pallas import tpu as pltpu
from jax.sharding import PartitionSpec as P

AXES = ("gx", "gy")
F32 = jnp.float32
BF16 = jnp.bfloat16
LOG2E = 1.4426950408889634
DIFFUSIVITY = 1.66
HEAT_FACTOR = 8.0
LANES = 128
HALF = 64
UNROLL_DOWN = 32
UNROLL_RISE = 32
UNROLL_TAU = 16
CHUNK = 256


def split3(x):
    hi = x.astype(BF16)
    rest = x - hi.astype(F32)
    mid = rest.astype(BF16)
    low = (rest - mid.astype(F32)).astype(BF16)
    return hi, mid, low


def dot(a, b, dims=((1,), (0,))):
    return lax.dot_general(a, b, (dims, ((), ())), preferred_element_type=F32)


def iota(shape, dim):
    return lax.broadcasted_iota(jnp.int32, shape, dim)


def fetch(pairs, sems):
    copies = [pltpu.make_async_copy(a, b, sems.at[i]) for i, (a, b) in enumerate(pairs)]
    for c in copies:
        c.start()
    for c in copies:
        c.wait()


def send_kernel(cos_hbm, day_hbm, alb_hbm, out_ref, cos_ref, day_ref, alb_ref, sems):
    fetch(((cos_hbm, cos_ref), (day_hbm, day_ref), (alb_hbm, alb_ref)), sems)
    rows = cos_ref.shape[0]
    devices = out_ref.shape[0]
    group = devices // rows
    per = LANES // group
    keep = iota((devices, LANES), 1) // per == iota((devices, LANES), 0) % group
    cosine = jnp.where(day_ref[...] == 1, cos_ref[...], 0.0)

    def spread(x):
        x = jnp.broadcast_to(x[:, None, :], (rows, group, LANES)).reshape(devices, LANES)
        return jnp.where(keep, x, 0.0)

    out_ref[...] = spread(cosine) + pltpu.roll(spread(alb_ref[...]), per, 1)


def predictor_kernel(
    state_hbm,
    kdist_hbm,
    ray_hbm,
    solar_hbm,
    span_hbm,
    out_ref,
    lhs_ref,
    tail_ref,
    rayh_ref,
    sun_ref,
    owner_ref,
    slot_ref,
    state_ref,
    kdist_ref,
    ray_ref,
    solar_ref,
    span_ref,
    sems,
):
    pairs = (
        (kdist_hbm, kdist_ref),
        (ray_hbm, ray_ref),
        (solar_hbm, solar_ref),
        (span_hbm, span_ref),
        (state_hbm, state_ref),
    )
    fetch(pairs, sems)
    fields, levels, columns = state_ref.shape
    gases = fields - 2
    devices = owner_ref.shape[0]
    span = span_ref[...]
    hot = jnp.where(iota((devices, columns), 0) == span // columns, 1.0, 0.0)
    owner_ref[...] = hot.astype(BF16)
    slot_ref[...] = span % (columns // devices)

    def level(l, _):
        t = state_ref[0, pl.ds(l, 1), :] / 250.0
        m = state_ref[1, pl.ds(l, 1), :]
        q = jnp.concatenate([state_ref[2 + i, pl.ds(l, 1), :] for i in range(gases)], 0)
        modes = (None, t, t * t, 1.0 / t)
        v = [(q if b == 0 else q * modes[b]) * m for b in range(4)]
        at = pl.multiple_of(l * 4 * gases, 4 * gases)
        out_ref[pl.ds(at, 4 * gases), :] = jnp.concatenate(v, 0).astype(BF16)
        return 0

    lax.fori_loop(0, levels, level, 0, unroll=2)
    base = 4 * gases * levels
    for j, term in enumerate(split3(state_ref[1])):
        out_ref[pl.ds(base + j * levels, levels), :] = term

    npred, points = kdist_ref.shape
    rows = points // 2
    lane_low = iota((1, LANES), 1) < HALF
    source, target = iota((npred, npred), 0), iota((npred, npred), 1)
    move = jnp.where(source == target % gases * 4 + target // gases, 1.0, 0.0).astype(BF16)
    scale = -DIFFUSIVITY * LOG2E
    k1, k2, _ = split3(scale * dot(kdist_ref[...], move, ((0,), (0,))))

    def column(ref):
        return jnp.broadcast_to(ref[...], (LANES, points)).T

    ray = scale * column(ray_ref)
    r1, r2, r3 = (x.astype(F32)[:, :16] for x in split3(ray))
    place = iota((points, 16), 1)
    r = jnp.where(place == 2, r3, 0.0)
    r = jnp.where(jnp.logical_or(place == 1, place == 4), r2, r)
    r = jnp.where(jnp.logical_or(jnp.logical_or(place == 0, place == 3), place == 5), r1, r)
    terms = jnp.concatenate([k1.astype(F32), k2.astype(F32), r], 1)
    low, high = terms[:rows], terms[rows:]
    lhs_ref[...] = terms.astype(BF16)
    tail_ref[...] = jnp.concatenate([low, high], 1).astype(BF16)

    for x, ref in ((0.5 * ray, rayh_ref), (column(solar_ref), sun_ref)):
        low, high = x[:rows], x[rows:]
        for k, y in enumerate((low, high, jnp.where(lane_low, low, high))):
            ref[2 * k] = y[: rows // 2]
            ref[2 * k + 1] = y[rows // 2 :]


def main_kernel(
    shift_ref,
    pred_ref,
    recv_ref,
    owner_ref,
    slot_ref,
    lhs_ref,
    tail_ref,
    rayh_ref,
    sun_ref,
    heat_ref,
    send_ref,
    extra_s,
    picked_s,
    mass_s,
    pick_s,
    rhs_s,
    aux_s,
    tau_s,
    half_s,
    trans_s,
    emit_s,
    back_s,
    net_s,
    sfc_s,
    out_s,
    fin_s,
):
    levels = heat_ref.shape[0]
    columns = pred_ref.shape[1]
    npred = pred_ref.shape[0] // levels - 3
    devices = recv_ref.shape[0]
    per = columns // devices
    part = rayh_ref.shape[1]
    base = npred * levels
    lane_low = iota((1, LANES), 1) < HALF
    half_rows = rhs_s.shape[2] // 2

    slot_hot = iota((per, columns), 0) == slot_ref[...]
    recv = pltpu.roll(recv_ref[...], shift_ref[0], 1).T[: 2 * per]
    sel = dot(jnp.concatenate(split3(recv), 0), owner_ref[...])
    sel = sel[: 2 * per] + sel[2 * per : 4 * per] + sel[4 * per :]
    cos_e = jnp.sum(jnp.where(slot_hot, sel[:per], 0.0), 0, keepdims=True)
    alb_e = jnp.sum(jnp.where(slot_hot, sel[per:], 0.0), 0, keepdims=True)
    extra = [x.astype(F32) for x in (*split3(cos_e), *split3(alb_e))]
    extra = jnp.concatenate(extra + [jnp.zeros((10, columns), F32)], 0)
    extra_s[...] = extra.astype(BF16)

    day = jnp.where(cos_e > 0.0, 1.0, 0.0)
    rows = columns // LANES
    day2 = jnp.concatenate([day[:, r * LANES : (r + 1) * LANES] for r in range(rows)], 0)
    upper = jnp.where(iota((LANES, LANES), 0) <= iota((LANES, LANES), 1), 1.0, 0.0)
    within = dot(day2.astype(BF16), upper.astype(BF16))
    place = []
    offset = jnp.zeros((1, 1), F32)
    for r in range(rows):
        place.append(within[r : r + 1] + offset)
        offset = offset + within[r : r + 1, LANES - 1 :]
    order = jnp.where(day > 0.0, jnp.concatenate(place, 1) - 1.0, -1.0).astype(jnp.int32)
    count = jnp.sum(day).astype(jnp.int32)
    before = [jnp.int32(0)]
    for k in range(columns // CHUNK):
        before.append(before[-1] + jnp.sum(day[:, k * CHUNK : (k + 1) * CHUNK]).astype(jnp.int32))
    chunks = (count + CHUNK - 1) // CHUNK
    units = (count + HALF - 1) // HALF

    def is_tail(unit):
        return jnp.logical_and(unit == units - 1, unit % 2 == 0)

    out_s[...] = jnp.zeros_like(out_s)
    fin_s[...] = jnp.zeros_like(fin_s)

    def gather(c, _):
        start = pl.multiple_of(c * CHUNK, CHUNK)
        hot = jnp.where(iota((CHUNK, columns), 0) + start == order, 1.0, 0.0).astype(BF16)
        pick_s[pl.ds(start, CHUNK), :] = hot
        for k in range(columns // CHUNK):
            at = slice(k * CHUNK, (k + 1) * CHUNK)

            def part_of():
                rows = jnp.concatenate([pred_ref[:, at], extra_s[:, at]], 0)
                return dot(rows, pick_s[pl.ds(start, CHUNK), at], ((1,), (1,)))

            @pl.when(jnp.logical_and(before[k] <= start, before[k + 1] > start))
            def _():
                picked_s[...] = part_of()

            @pl.when(jnp.logical_and(before[k] > start, before[k] < start + CHUNK))
            def _():
                picked_s[...] += part_of()

        sub = iota((16, LANES), 0)
        for j in range(CHUNK // LANES):
            chunk = c * (CHUNK // LANES) + j
            lanes = slice(j * LANES, (j + 1) * LANES)
            piece = picked_s.at[:, lanes]
            ms = [piece[base + k * levels : base + (k + 1) * levels, :] for k in range(3)]
            for k in range(3):
                mass_s[k] = ms[k]
            ex = piece[base + 3 * levels : base + 3 * levels + 8, :]
            cosine = ex[0:1] + ex[1:2] + ex[2:3]
            albedo = ex[3:4] + ex[4:5] + ex[5:6]
            aux = jnp.concatenate(
                [ms[0] + ms[1] + ms[2], cosine, albedo, jnp.ones((6, LANES), F32)], 0
            )
            tail = is_tail(2 * chunk)
            aux_s[chunk] = jnp.where(
                jnp.logical_or(lane_low, jnp.logical_not(tail)), aux, pltpu.roll(aux, HALF, 1)
            )
            for l in range(levels):
                x = piece[l * npred : (l + 1) * npred, :].astype(BF16)
                rows = [mass_s[k, pl.ds(l, 1), :] for k in range(3)]
                y = jnp.where(sub < 3, rows[0], jnp.where(sub < 5, rows[1], rows[2]))
                y = jnp.where(sub < 6, y, 0.0).astype(BF16)
                at = pl.ds(l % 2 * LANES, LANES)
                rhs_s[chunk, l // 2, pl.ds(0, npred), at] = x
                rhs_s[chunk, l // 2, pl.ds(npred, npred), at] = x
                rhs_s[chunk, l // 2, pl.ds(2 * npred, 16), at] = y

            @pl.when(tail)
            def _():
                def pair(l, _):
                    for j in range(2):
                        at = pl.ds(j * LANES, LANES)
                        x = rhs_s[chunk, l, pl.ds(npred, npred + 16), at].astype(F32)
                        x = pltpu.roll(x, HALF, 1).astype(BF16)
                        rhs_s[chunk, l, pl.ds(half_rows, npred), at] = x[:npred]
                        rhs_s[chunk, l, pl.ds(half_rows + npred, npred + 16), at] = x
                    return 0

                lax.fori_loop(0, levels // 2, pair, 0, unroll=2)

        return 0

    lax.fori_loop(0, chunks, gather, 0)

    def fold(x):
        return jnp.sum(x.reshape(x.shape[0] // 8, 8, LANES), 0)

    def where_is(unit):
        kind = jnp.where(is_tail(unit), 2, unit % 2)
        return unit // 2, kind

    def one(unit, slot):
        chunk, kind = where_is(unit)
        g = 2 * kind + slot
        now = tau_s.at[2 * (kind % 2) + slot]
        half = half_s.at[2 * (kind % 2) + slot]
        cosine = aux_s[chunk, pl.ds(levels, 1), :]
        albedo = aux_s[chunk, pl.ds(levels + 1, 1), :]
        slope = 1.0 / (DIFFUSIVITY * cosine)

        if slot == 0:

            def keep(l, out, first):
                for j in range(2):
                    mass = aux_s[chunk, pl.ds(2 * l + j, 1), :]
                    for s in range(out.shape[0] // part):
                        y = out[s * part : (s + 1) * part, j * LANES : (j + 1) * LANES]
                        tau_s[s, 2 * l + j] = y
                        half_s[s, 2 * l + j] = rayh_ref[first + s] * mass * pl.reciprocal(y)
                return 0

            @pl.when(kind == 0)
            def _():
                def pair(l, _):
                    return keep(l, dot(lhs_ref[...], rhs_s[chunk, l, :half_rows]), 0)

                lax.fori_loop(0, levels // 2, pair, 0, unroll=UNROLL_TAU)

            @pl.when(kind == 2)
            def _():
                def pair(l, _):
                    return keep(l, dot(tail_ref[...], rhs_s[chunk, l]), 4)

                lax.fori_loop(0, levels // 2, pair, 0, unroll=UNROLL_TAU)

            @pl.when(kind != 1)
            def _():
                net_s[...] = jnp.zeros_like(net_s)
                sfc_s[...] = jnp.zeros_like(sfc_s)

        def down(l, carry):
            back, emit, direct = carry
            net_s[l] += fold(direct + emit)
            tau = now[l]
            ext = jnp.exp2(tau)
            beam = jnp.exp2(tau * slope)
            half_w = half[l]
            reflect = half_w * (1.0 - ext)
            transmit = ext + reflect
            lower = direct * beam
            source = half_w * (direct - lower)
            inv = pl.reciprocal(1.0 - reflect * back)
            trans = transmit * inv
            trans_s[l] = trans
            emit_s[l] = (source + reflect * emit) * inv
            back_s[l] = back
            new_back = reflect + (transmit * back) * trans
            new_emit = source + trans * (emit + back * source)
            return new_back, new_emit, lower

        zero = jnp.zeros((part, LANES), F32)
        back, emit, direct = lax.fori_loop(
            0, levels, down, (zero, zero, sun_ref[g] * cosine), unroll=UNROLL_DOWN
        )
        up = albedo * (emit + direct) * pl.reciprocal(1.0 - albedo * back)
        dif = emit + back * up
        sfc_s[0] += fold(direct)
        sfc_s[1] += fold(dif)
        net_s[levels] += fold(direct + dif - up)

        def rise(j, up):
            l = levels - 1 - j
            up = trans_s[l] * up + emit_s[l]
            net_s[l] -= fold(up - back_s[l] * up)
            return up

        up = lax.fori_loop(0, levels, rise, up, unroll=UNROLL_RISE)
        sfc_s[2] += fold(up)

        if slot == 0:
            return

        @pl.when(kind != 0)
        def _():
            net = jnp.sum(net_s[...], 1)
            heat = HEAT_FACTOR * (net[:levels] - net[1:])
            out = jnp.concatenate([heat, jnp.sum(sfc_s[...], 1), jnp.zeros((5, LANES), F32)], 0)
            out = jnp.where(kind == 2, out + pltpu.roll(out, HALF, 1), out)
            mass = aux_s[chunk, pl.ds(0, levels), :]
            out = out / jnp.concatenate([mass, jnp.ones((8, LANES), F32)], 0)
            out_s[chunk] = jnp.where(iota((1, LANES), 1) + chunk * LANES < count, out, 0.0)

    def both(unit, _):
        one(unit, 0)
        one(unit, 1)
        return 0

    lax.fori_loop(0, units, both, 0)

    def spread(c, _):
        two = jnp.concatenate([out_s[(CHUNK // LANES) * c + j] for j in range(CHUNK // LANES)], 1)
        rows = two.shape[0]
        back = dot(
            jnp.concatenate([x.astype(F32) for x in split3(two)], 0).astype(BF16),
            pick_s[pl.ds(pl.multiple_of(c * CHUNK, CHUNK), CHUNK), :],
        )
        fin_s[...] += back[:rows] + back[rows : 2 * rows] + back[2 * rows :]
        return 0

    lax.fori_loop(0, chunks, spread, 0)

    heat_ref[...] = fin_s[pl.ds(0, levels), :]
    sfc = fin_s[pl.ds(levels, 8), :]
    vals = jnp.concatenate([jnp.where(slot_hot, sfc[q : q + 1], 0.0) for q in range(3)], 0)
    hot = owner_ref[...]
    terms = jnp.concatenate([x.astype(F32) for x in split3(vals)], 0).astype(BF16)
    send = dot(hot, terms, ((1,), (1,)))
    send = sum(send[:, j * 3 * per : (j + 1) * 3 * per] for j in range(3))
    send_ref[...] = jnp.concatenate([send, jnp.zeros((devices, LANES - 3 * per), F32)], 1)


def recv_kernel(recv_ref, out_ref):
    devices = recv_ref.shape[0]
    width = out_ref.shape[1]
    per = width // devices
    group = LANES // per
    lane = iota((LANES, 3 * LANES), 1)
    hot = jnp.where(iota((LANES, 3 * LANES), 0) == lane // LANES * per + lane % per, 1.0, 0.0)
    hot = hot.astype(BF16)
    x = sum(dot(term, hot) for term in split3(recv_ref[...]))
    shape = (devices, 3 * LANES)
    x = jnp.where(iota(shape, 1) % LANES // per == iota(shape, 0) % group, x, 0.0)
    x = jnp.sum(x.reshape(devices // group, group, 3 * LANES), 1)
    for q in range(3):
        for r in range(devices // group):
            out_ref[q : q + 1, r * LANES : (r + 1) * LANES] = x[
                r : r + 1, q * LANES : (q + 1) * LANES
            ]


def exchange(x):
    rows = x.shape[0]
    y = lax.all_to_all(
        x.reshape(rows, 1, LANES), AXES, split_axis=0, concat_axis=0, tiled=True
    )
    return y.reshape(rows, LANES)


def in_hbm(x):
    return pltpu.with_memory_space_constraint(x, pltpu.HBM)


def local(state, kdist, rayleigh, solar, span_map, cos_zenith, day_flag, albedo):
    fields, levels, columns = state.shape
    devices = lax.axis_size(AXES)
    per = columns // devices
    group = LANES // per
    rows = columns // LANES
    npred = kdist.shape[1]
    grows = kdist.shape[0] // 2

    hbm = pl.BlockSpec(memory_space=pltpu.HBM)
    sent = pl.pallas_call(
        send_kernel,
        out_shape=jax.ShapeDtypeStruct((devices, LANES), F32),
        in_specs=[hbm] * 3,
        scratch_shapes=[
            pltpu.VMEM((rows, LANES), F32),
            pltpu.VMEM((rows, LANES), jnp.int32),
            pltpu.VMEM((rows, LANES), F32),
            pltpu.SemaphoreType.DMA((3,)),
        ],
        compiler_params=pltpu.CompilerParams(vmem_limit_bytes=4 << 20),
        name="send",
    )(
        in_hbm(cos_zenith.reshape(rows, LANES)),
        in_hbm(day_flag.reshape(rows, LANES)),
        in_hbm(albedo.reshape(rows, LANES)),
    )
    recv = exchange(sent)
    points = 2 * grows
    preds, lhs, tail, rayh, sun, owner, slot = pl.pallas_call(
        predictor_kernel,
        out_shape=(
            jax.ShapeDtypeStruct(((npred + 3) * levels, columns), BF16),
            jax.ShapeDtypeStruct((points, 2 * npred + 16), BF16),
            jax.ShapeDtypeStruct((grows, 4 * npred + 32), BF16),
            jax.ShapeDtypeStruct((6, grows // 2, LANES), F32),
            jax.ShapeDtypeStruct((6, grows // 2, LANES), F32),
            jax.ShapeDtypeStruct((devices, columns), BF16),
            jax.ShapeDtypeStruct((1, columns), jnp.int32),
        ),
        in_specs=[hbm] * 5,
        scratch_shapes=[
            pltpu.VMEM((fields, levels, columns), F32),
            pltpu.VMEM((npred, points), BF16),
            pltpu.VMEM((1, points), F32),
            pltpu.VMEM((1, points), F32),
            pltpu.VMEM((1, columns), jnp.int32),
            pltpu.SemaphoreType.DMA((5,)),
        ],
        compiler_params=pltpu.CompilerParams(vmem_limit_bytes=12 << 20),
        name="predictors",
    )(
        in_hbm(state),
        in_hbm(kdist.T),
        in_hbm(rayleigh.reshape(1, -1)),
        in_hbm(solar.reshape(1, -1)),
        in_hbm(span_map.reshape(1, columns)),
    )
    shift = (LANES - lax.axis_index(AXES) % group * per) % LANES
    chunks = columns // LANES
    g_array = pltpu.VMEM((levels, grows // 2, LANES), F32)
    vmem = pl.BlockSpec(memory_space=pltpu.VMEM)
    heating, back = pl.pallas_call(
        main_kernel,
        out_shape=(
            jax.ShapeDtypeStruct((levels, columns), F32),
            jax.ShapeDtypeStruct((devices, LANES), F32),
        ),
        in_specs=[pl.BlockSpec(memory_space=pltpu.SMEM)] + [vmem] * 8,
        out_specs=(vmem, vmem),
        scratch_shapes=[
            pltpu.VMEM((16, columns), BF16),
            pltpu.VMEM(((npred + 3) * levels + 16, CHUNK), F32),
            pltpu.VMEM((3, levels, LANES), F32),
            pltpu.VMEM((columns, columns), BF16),
            pltpu.VMEM((chunks, levels // 2, tail.shape[1], 2 * LANES), BF16),
            pltpu.VMEM((chunks, levels + 8, LANES), F32),
            pltpu.VMEM((4, levels, grows // 2, LANES), F32),
            pltpu.VMEM((4, levels, grows // 2, LANES), F32),
            g_array,
            g_array,
            g_array,
            pltpu.VMEM((levels + 1, 8, LANES), F32),
            pltpu.VMEM((3, 8, LANES), F32),
            pltpu.VMEM((chunks, levels + 8, LANES), F32),
            pltpu.VMEM((levels + 8, columns), F32),
        ],
        compiler_params=pltpu.CompilerParams(vmem_limit_bytes=34 << 20),
        name="physics",
    )(
        shift.reshape(1).astype(jnp.int32),
        preds,
        recv,
        owner,
        slot,
        lhs,
        tail,
        rayh,
        sun,
    )
    surface = pl.pallas_call(
        recv_kernel,
        out_shape=jax.ShapeDtypeStruct((3, columns), F32),
        compiler_params=pltpu.CompilerParams(vmem_limit_bytes=4 << 20),
        name="receive",
    )(exchange(back))
    return heating, surface


def solution(mesh):
    cols = P(AXES)
    in_specs = (P(None, None, AXES), P(), P(), P(), cols, cols, cols, cols)
    out_specs = (P(None, AXES), P(None, AXES))
    return jax.shard_map(
        local, mesh=mesh, in_specs=in_specs, out_specs=out_specs, check_vma=False
    )
```
